512 devices in a mesh: row: 32 (over y_lo, z), col: 16 (over y_hi, x, core).
Axes of the slice: x: 4, y: 8 (y_hi: 2, y_lo: 4; y = y_hi * 4 + y_lo), z: 8, core: 2. Of those that a mesh axis runs over, the one named last changes fastest.
Arguments:
- amplitudes: bfloat16 [65536, 16384], P(('row', 'col')), may hold values from -6 to 6
- amp_tiles: int32 [1024, 256], P(('row', 'col')), may hold values 0 or 1
- integrals: bfloat16 [512, 16384], P('row', 'col'), may hold values from -0.046875 to 0.046875
- int_tiles: int32 [8, 256], P(None, 'col'), may hold values 0 or 1
Outputs:
- ladder: bfloat16 [512, 65536], P('col', 'row')
The draws below stay inside these ranges and needn't reach their ends.
All inputs are finite; a program needn't handle non-finite values. No bound on the sum of `amp_tiles` or of `int_tiles` on one device may be relied on, other than what follows from the above.
Results may differ from the reference program's by a relative error of at most 0.001.
Values may be sent and summed in bfloat16 or wider, within the bound.
No kernel may reach another device: no remote copies, remote signals or barrier semaphores. Data moves between devices by JAX's collectives and lax.ppermute only.
A program may use at most 64 MiB of HBM per device.

```python
import jax
import jax.numpy as jnp
from jax import lax

TILE = 64
K = 16384
A = 512
P_SIZE = 65536
N_ROW = 32


def set_ends(values, own_key, least, largest):
    extent = values.shape
    place = [jax.random.randint(jax.random.fold_in(own_key, axis), (), 0, extent[axis]) for axis in range(len(extent))]
    values = values.at[tuple(place)].set(least)
    longest = extent.index(max(extent))
    place[longest] = (place[longest] + 1) % extent[longest]
    return values.at[tuple(place)].set(largest)


def shard_levels(key, shape, shards, least, largest):
    loudness = 1.0
    for position, parts in shards:
        steps = jax.random.uniform(jax.random.fold_in(jax.random.fold_in(key, 6), position), (parts,), jnp.float32, least / len(shards), largest / len(shards))
        loudness = loudness * jnp.repeat(jnp.exp(steps), shape[position] // parts).reshape((-1,) + (1,) * (len(shape) - 1 - position))
    return loudness


def bell_draw(stream_key, extent, spread, most, cuts=(), kind=jnp.bfloat16):
    array = spread * jax.random.normal(stream_key, extent, jnp.float32)
    if cuts:
        array = array * shard_levels(stream_key, extent, cuts, -0.22, 0.18)
    return jnp.clip(array, -most, most).astype(kind)


def setup_inputs(seed: int = 0) -> dict:
    keys = jax.random.split(jax.random.key(seed), 5)
    return {
        "amplitudes": bell_draw(keys[0], (P_SIZE, K), 1.0, 6.0, ((0, 512),)),
        "amp_tiles": set_ends((jax.random.randint(keys[1], (P_SIZE // TILE, K // TILE), 0, 4) < 3).astype(jnp.int32), jax.random.fold_in(keys[1], 1), 0, 1),
        "integrals": bell_draw(keys[2], (A, K), K ** -0.5, 0.046875, ((0, 32), (1, 16))),
        "int_tiles": set_ends((jax.random.randint(keys[3], (A // TILE, K // TILE), 0, 4) < 3).astype(jnp.int32), jax.random.fold_in(keys[3], 1), 0, 1),
    }


def expand_mask(tiles):
    return jnp.repeat(jnp.repeat(tiles, TILE, axis=0), TILE, axis=1).astype(jnp.bfloat16)


def reference(amplitudes, amp_tiles, integrals, int_tiles):
    stored_ints = integrals * expand_mask(int_tiles)
    amp_blocks = amplitudes.reshape(N_ROW, P_SIZE // N_ROW, K)
    tile_blocks = amp_tiles.reshape(N_ROW, P_SIZE // N_ROW // TILE, K // TILE)

    def block_ladder(operands):
        amplitude_block, tile_block = operands
        stored_amps = amplitude_block * expand_mask(tile_block)
        result = lax.dot_general(stored_ints, stored_amps, (((1,), (1,)), ((), ())), preferred_element_type=jnp.float32)
        return result.astype(jnp.bfloat16)

    blocks = lax.map(block_ladder, (amp_blocks, tile_blocks))
    return jnp.transpose(blocks, (1, 0, 2)).reshape(A, P_SIZE)
```

```python
import jax
import jax.numpy as jnp
from jax import lax
from jax.experimental import pallas as pl
from jax.experimental.pallas import tpu as pltpu
from jax.sharding import Mesh, PartitionSpec as P

TILE = 64
YLO, Z, YHI, X, CORE = 4, 8, 2, 4, 2
Y = YHI * YLO
KB = YHI * X
PANEL = 1024
ROWS = 16
PAIRS = 128
ALL = ("ylo", "z", "yhi", "x", "core")
HALF = 16


def place(ylo, z, yhi, x, core):
    return (((ylo * Z + z) * YHI + yhi) * X + x) * CORE + core


def plane_groups():
    groups = []
    for z in range(Z):
        groups.append([place(y % YLO, z, y // YLO, x, 0) for x in range(X) for y in range(Y)])
    for y in range(Y):
        groups.append([place(y % YLO, z, y // YLO, x, 1) for x in range(X) for z in range(Z)])
    return groups


def ring_pairs(step):
    pairs = []
    for x in range(X):
        for y in range(Y):
            for z in range(Z):
                to_z, to_y = (z + step) % Z, (y + step) % Y
                pairs.append((place(y % YLO, z, y // YLO, x, 0), place(y % YLO, to_z, y // YLO, x, 0)))
                pairs.append((place(y % YLO, z, y // YLO, x, 1), place(to_y % YLO, z, to_y // YLO, x, 1)))
    return sorted(pairs)


def spread(tiles):
    tile = lax.broadcasted_iota(jnp.int32, (PANEL // TILE, PANEL), 0)
    lane = lax.broadcasted_iota(jnp.int32, (PANEL // TILE, PANEL), 1)
    picks = (lane // TILE == tile).astype(jnp.bfloat16)
    flags = tiles.astype(jnp.float32).astype(jnp.bfloat16)
    return jnp.dot(flags, picks, preferred_element_type=jnp.float32)


def integral_kernel(meta, ints_ref, tiles_ref, out_ref):
    wanted = lax.broadcasted_iota(jnp.int32, (8, PANEL // TILE), 0) == meta[2]
    row = jnp.sum(jnp.where(wanted, tiles_ref[...], 0), axis=0, keepdims=True)
    flags = spread(jnp.broadcast_to(row, (8, PANEL // TILE)))[:1]
    masked = (ints_ref[...].astype(jnp.float32) * flags).astype(jnp.bfloat16)
    out_ref[...] = jnp.broadcast_to(masked[None], out_ref.shape)


def split_kernel(meta, own_ref, other_ref, own_tiles, other_tiles, keep_ref, send_ref):
    for values, tiles, out in ((own_ref, own_tiles, keep_ref), (other_ref, other_tiles, send_ref)):
        flags = spread(tiles[0])
        for part in range(PAIRS // TILE):
            rows = pl.ds(part * TILE, TILE)
            out[0, rows, :] = (values[rows, :].astype(jnp.float32) * flags[part : part + 1]).astype(jnp.bfloat16)


def split_amplitudes(meta, amplitudes, amp_tiles):
    tiles = amp_tiles.reshape(PAIRS // TILE, KB * CORE, PANEL // TILE).transpose(1, 0, 2)
    block = (PAIRS, PANEL)
    tile_block = (1, PAIRS // TILE, PANEL // TILE)
    shape = jax.ShapeDtypeStruct((KB, PAIRS, PANEL), jnp.bfloat16)
    return pl.pallas_call(
        split_kernel,
        grid_spec=pltpu.PrefetchScalarGridSpec(
            num_scalar_prefetch=1,
            grid=(KB,),
            in_specs=[
                pl.BlockSpec(block, lambda i, m: (0, 2 * i + m[0])),
                pl.BlockSpec(block, lambda i, m: (0, 2 * i + 1 - m[0])),
                pl.BlockSpec(tile_block, lambda i, m: (2 * i + m[0], 0, 0)),
                pl.BlockSpec(tile_block, lambda i, m: (2 * i + 1 - m[0], 0, 0)),
            ],
            out_specs=[pl.BlockSpec((1, PAIRS, PANEL), lambda i, m: (i, 0, 0))] * 2,
        ),
        out_shape=(shape, shape),
        compiler_params=pltpu.CompilerParams(vmem_limit_bytes=16 << 20),
        cost_estimate=pl.CostEstimate(flops=8 << 20, bytes_accessed=8 << 20, transcendentals=0),
        name="split_amplitudes",
    )(meta, amplitudes, amplitudes, tiles, tiles)


SLOTS = [(0, 0), (0, 1)] + [(s, h) for s in (-1, 1, -2, 2, -3, 3) for h in (0, 1)] + [(4, 0), (4, 1)]


def ladder_kernel(meta, *refs):
    blocks, own, other = refs[: len(SLOTS)], refs[len(SLOTS)], refs[len(SLOTS) + 1]
    keep_ref, send_ref, ints, amps, total, sem = refs[len(SLOTS) + 2 :]
    core, here = meta[0], meta[1]

    def copies(on):
        found = []
        for source, (offset, half) in zip(blocks, SLOTS, strict=True):
            there = lax.rem(here + offset + 8, 8)
            for m in range(2):
                x = half * 2 + m
                if on == 0:
                    for yhi in range(YHI):
                        found.append((source.at[pl.ds(m * 8 + yhi * YLO, YLO)], ints.at[yhi * X + x, :, there]))
                else:
                    found.append((source.at[pl.ds(m * 8, Z)], ints.at[(there // YLO) * X + x, lax.rem(there, YLO)]))
        return [pltpu.make_async_copy(a, b, sem.at[0]) for a, b in found]

    mine = [
        pltpu.make_async_copy(own, amps.at[:, pl.ds(pl.multiple_of(core * PAIRS, PAIRS), PAIRS)], sem.at[0]),
        pltpu.make_async_copy(other, amps.at[:, pl.ds(pl.multiple_of((1 - core) * PAIRS, PAIRS), PAIRS)], sem.at[0]),
    ]
    for copy in mine:
        copy.start()
    for on in range(2):

        @pl.when(core == on)
        def _():
            todo = copies(on)
            for copy in todo:
                copy.start()
            for copy in todo:
                copy.wait()

    for copy in mine:
        copy.wait()
    for panel in range(KB):
        product = lax.dot_general(
            ints[panel].reshape(YLO * Z * ROWS, PANEL),
            amps[panel],
            (((1,), (1,)), ((), ())),
            preferred_element_type=jnp.float32,
        ).reshape(total.shape)
        if panel == 0:
            total[...] = product
        else:
            total[...] += product
    keep_ref[...] = total[:, core]
    send_ref[...] = total[:, 1 - core]


def local(amplitudes, amp_tiles, integrals, int_tiles):
    core = lax.axis_index("core")
    z = lax.axis_index("z")
    ylo = lax.axis_index("ylo")
    y = lax.axis_index("yhi") * YLO + ylo
    meta = jnp.stack([core, jnp.where(core == 0, z, y), (ylo * Z + z) // 4]).astype(jnp.int32)

    panels = pl.pallas_call(
        integral_kernel,
        in_specs=[pl.BlockSpec(memory_space=pltpu.SMEM)] + [pl.BlockSpec(memory_space=pltpu.VMEM)] * 2,
        out_specs=pl.BlockSpec(memory_space=pltpu.VMEM),
        out_shape=jax.ShapeDtypeStruct((X * Y, ROWS, PANEL), jnp.bfloat16),
        compiler_params=pltpu.CompilerParams(vmem_limit_bytes=8 << 20),
        name="mask_integrals",
    )(meta, integrals, int_tiles)
    plane = lax.all_to_all(panels, ALL, 0, 0, axis_index_groups=plane_groups(), tiled=True)

    own, other = split_amplitudes(meta, amplitudes, amp_tiles)
    other = lax.ppermute(other, "core", [(0, 1), (1, 0)])

    up, down = ring_pairs(1), ring_pairs(-1)
    have = {(0, 0): plane[:HALF], (0, 1): plane[HALF:]}
    for step in (1, 2, 3):
        for half in (0, 1):
            have[-step, half] = lax.ppermute(have[-step + 1, half], ALL, up)
            have[step, half] = lax.ppermute(have[step - 1, half], ALL, down)
    have[4, 0] = lax.ppermute(have[-3, 0], ALL, up)
    have[4, 1] = lax.ppermute(have[3, 1], ALL, down)

    half_sum = jax.ShapeDtypeStruct((KB, 32, CORE * PAIRS), jnp.float32)
    keep, send = pl.pallas_call(
        ladder_kernel,
        in_specs=[pl.BlockSpec(memory_space=pltpu.SMEM)] + [pl.BlockSpec(memory_space=pl.ANY)] * (len(SLOTS) + 2),
        out_specs=[pl.BlockSpec(memory_space=pltpu.VMEM)] * 2,
        out_shape=(half_sum, half_sum),
        scratch_shapes=[
            pltpu.VMEM((KB, YLO, Z, ROWS, PANEL), jnp.bfloat16),
            pltpu.VMEM((KB, CORE * PAIRS, PANEL), jnp.bfloat16),
            pltpu.VMEM((KB, CORE, 32, CORE * PAIRS), jnp.float32),
            pltpu.SemaphoreType.DMA((1,)),
        ],
        compiler_params=pltpu.CompilerParams(vmem_limit_bytes=24 << 20),
        cost_estimate=pl.CostEstimate(flops=2 << 30, bytes_accessed=13 << 20, transcendentals=0),
        name="ladder",
    )(meta, *[have[slot] for slot in SLOTS], own, other)
    got = lax.ppermute(send, "core", [(0, 1), (1, 0)])
    summed = (keep + got).astype(jnp.bfloat16)
    pieces = lax.all_to_all(summed, ("yhi", "x"), 0, 0, tiled=True)
    return pieces.transpose(1, 0, 2).reshape(32, KB * CORE * PAIRS)


def solution(mesh):
    grid = Mesh(mesh.devices.reshape(YLO, Z, YHI, X, CORE), ALL)
    rows, cols = ("ylo", "z"), ("yhi", "x", "core")
    return jax.shard_map(
        local,
        mesh=grid,
        in_specs=(P(ALL, None), P(ALL, None), P(rows, cols), P(None, cols)),
        out_specs=P(cols, rows),
        check_vma=False,
    )
```

```python
import jax
import jax.numpy as jnp
from jax import lax
from jax.experimental import pallas as pl
from jax.experimental.pallas import tpu as pltpu
from jax.sharding import Mesh, PartitionSpec as P

TILE = 64
YLO, Z, YHI, XH, XP, CORE = 4, 8, 2, 2, 2, 2
Y = YHI * YLO
QUADS = YHI * XH
PANEL = 1024
ROWS = 16
PAIRS = 128
TEAM = XP * CORE
ALL = ("ylo", "z", "yhi", "xh", "xp", "core")


def place(y, z, xh, xp, core):
    return ((((y % YLO * Z + z) * YHI + y // YLO) * XH + xh) * XP + xp) * CORE + core


def plane_groups():
    groups = []
    for xp in range(XP):
        groups += [[place(y, z, xh, xp, 0) for xh in range(XH) for y in range(Y)] for z in range(Z)]
        groups += [[place(y, z, xh, xp, 1) for xh in range(XH) for z in range(Z)] for y in range(Y)]
    return groups


def ring_pairs(step):
    pairs = []
    for xh in range(XH):
        for xp in range(XP):
            for y in range(Y):
                for z in range(Z):
                    pairs.append((place(y, z, xh, xp, 0), place(y, (z + step) % Z, xh, xp, 0)))
                    pairs.append((place(y, z, xh, xp, 1), place((y + step) % Y, z, xh, xp, 1)))
    return sorted(pairs)


def spread(tiles):
    tile = lax.broadcasted_iota(jnp.int32, (PANEL // TILE, PANEL), 0)
    lane = lax.broadcasted_iota(jnp.int32, (PANEL // TILE, PANEL), 1)
    picks = (lane // TILE == tile).astype(jnp.bfloat16)
    flags = tiles.astype(jnp.float32).astype(jnp.bfloat16)
    return jnp.dot(flags, picks, preferred_element_type=jnp.float32)


def integral_kernel(meta, ints_hbm, tiles_hbm, out_ref, ints, tiles, sem):
    copies = [
        pltpu.make_async_copy(ints_hbm, ints, sem.at[0]),
        pltpu.make_async_copy(tiles_hbm, tiles, sem.at[1]),
    ]
    for copy in copies:
        copy.start()
    for copy in copies:
        copy.wait()
    wanted = lax.broadcasted_iota(jnp.int32, (8, PANEL // TILE), 0) == meta[2]
    row = jnp.sum(jnp.where(wanted, tiles[...], 0), axis=0, keepdims=True)
    flags = spread(jnp.broadcast_to(row, (8, PANEL // TILE)))[:1]
    masked = (ints[...].astype(jnp.float32) * flags).astype(jnp.bfloat16)
    out_ref[...] = jnp.broadcast_to(masked[None], out_ref.shape)


def split_kernel(meta, *refs):
    own, swap, across = refs[2 * TEAM :]
    outs = (own.at[0], swap.at[0], across.at[0, 0], across.at[1, 0])
    for values, tiles, out in zip(refs[:TEAM], refs[TEAM : 2 * TEAM], outs, strict=True):
        flags = spread(tiles[0])
        for part in range(PAIRS // TILE):
            rows = pl.ds(part * TILE, TILE)
            out[rows, :] = (values[rows, :].astype(jnp.float32) * flags[part : part + 1]).astype(jnp.bfloat16)


def split_amplitudes(meta, amplitudes, amp_tiles):
    tiles = amp_tiles.reshape(PAIRS // TILE, QUADS * TEAM, PANEL // TILE).transpose(1, 0, 2)

    def values(n):
        return pl.BlockSpec((PAIRS, PANEL), lambda i, m: (0, TEAM * i + (m[3] ^ n)))

    def flags(n):
        return pl.BlockSpec((1, PAIRS // TILE, PANEL // TILE), lambda i, m: (TEAM * i + (m[3] ^ n), 0, 0))

    block = pl.BlockSpec((1, PAIRS, PANEL), lambda i, m: (i, 0, 0))
    shape = (QUADS, PAIRS, PANEL)
    return pl.pallas_call(
        split_kernel,
        grid_spec=pltpu.PrefetchScalarGridSpec(
            num_scalar_prefetch=1,
            grid=(QUADS,),
            in_specs=[values(n) for n in range(TEAM)] + [flags(n) for n in range(TEAM)],
            out_specs=[block, block, pl.BlockSpec((CORE, 1, PAIRS, PANEL), lambda i, m: (0, i, 0, 0))],
        ),
        out_shape=[jax.ShapeDtypeStruct(s, jnp.bfloat16) for s in (shape, shape, (CORE,) + shape)],
        compiler_params=pltpu.CompilerParams(vmem_limit_bytes=60 << 20),
        cost_estimate=pl.CostEstimate(flops=8 << 20, bytes_accessed=8 << 20, transcendentals=0),
        name="split_amplitudes",
    )(meta, *[amplitudes] * TEAM, *[tiles] * TEAM)


MEMBERS = XH * 8
SLOTS = [(offset, 0, MEMBERS) for offset in (0, -1, 1, -2, 2, -3, 3)] + [(4, 0, 8), (4, 8, 8)]


def ladder_kernel(meta, *refs):
    blocks, team = refs[: len(SLOTS)], refs[len(SLOTS) : len(SLOTS) + TEAM]
    keep_ref, send_ref, ints, amps, total, sem = refs[len(SLOTS) + TEAM :]
    core, here, me = meta[0], meta[1], meta[3]
    xp = me // CORE

    def copies(on):
        found = []
        for source, (offset, first, members) in zip(blocks, SLOTS, strict=True):
            there = lax.rem(here + offset + 8, 8)
            for xh in range(first // 8, (first + members) // 8):
                at = xh * 8 - first
                if on == 0:
                    for yhi in range(YHI):
                        found.append((source.at[pl.ds(at + yhi * YLO, YLO)], ints.at[yhi * XH + xh, :, there]))
                else:
                    found.append((source.at[pl.ds(at, Z)], ints.at[(there // YLO) * XH + xh, lax.rem(there, YLO)]))
        return [pltpu.make_async_copy(a, b, sem.at[0]) for a, b in found]

    mine = []
    for n in range(TEAM):
        rows = pl.ds(pl.multiple_of((me ^ n) * PAIRS, PAIRS), PAIRS)
        source = team[n].at[0] if n == 2 else team[n]
        mine.append(pltpu.make_async_copy(source, amps.at[:, rows], sem.at[0]))
    for copy in mine:
        copy.start()
    for on in range(CORE):

        @pl.when(core == on)
        def _():
            todo = copies(on)
            for copy in todo:
                copy.start()
            for copy in todo:
                copy.wait()

    for copy in mine:
        copy.wait()
    for panel in range(QUADS):
        product = lax.dot_general(
            ints[panel].reshape(YLO * Z * ROWS, PANEL),
            amps[panel],
            (((1,), (1,)), ((), ())),
            preferred_element_type=jnp.float32,
        ).reshape(total.shape)
        if panel == 0:
            total[...] = product
        else:
            total[...] += product
    for n in range(XP):
        keep_ref[n] = total[:, (xp ^ n) * CORE + core]
        send_ref[n] = total[:, (xp ^ n) * CORE + 1 - core]


def compute(amplitudes, amp_tiles, integrals, int_tiles):
    core = lax.axis_index("core")
    z = lax.axis_index("z")
    ylo = lax.axis_index("ylo")
    y = lax.axis_index("yhi") * YLO + ylo
    me = lax.axis_index("xp") * CORE + core
    meta = jnp.stack([core, jnp.where(core == 0, z, y), (ylo * Z + z) // 4, me]).astype(jnp.int32)

    panels = pl.pallas_call(
        integral_kernel,
        in_specs=[pl.BlockSpec(memory_space=pltpu.SMEM)] + [pl.BlockSpec(memory_space=pltpu.HBM)] * 2,
        out_specs=pl.BlockSpec(memory_space=pltpu.VMEM),
        out_shape=jax.ShapeDtypeStruct((MEMBERS, ROWS, PANEL), jnp.bfloat16),
        scratch_shapes=[
            pltpu.VMEM((ROWS, PANEL), jnp.bfloat16),
            pltpu.VMEM((8, PANEL // TILE), jnp.int32),
            pltpu.SemaphoreType.DMA((2,)),
        ],
        compiler_params=pltpu.CompilerParams(vmem_limit_bytes=60 << 20),
        name="mask_integrals",
    )(meta, integrals, int_tiles)
    plane = lax.all_to_all(panels, ALL, 0, 0, axis_index_groups=plane_groups(), tiled=True)

    own, swap, across = split_amplitudes(meta, amplitudes, amp_tiles)
    across = lax.ppermute(across, "xp", [(0, 1), (1, 0)])
    swap = lax.ppermute(swap, "core", [(0, 1), (1, 0)])
    relay = lax.ppermute(across[1], "core", [(0, 1), (1, 0)])

    up, down = ring_pairs(1), ring_pairs(-1)
    have = {0: plane}
    for step in (1, 2, 3):
        have[-step] = lax.ppermute(have[1 - step], ALL, up)
        have[step] = lax.ppermute(have[step - 1], ALL, down)
    last_up = lax.ppermute(have[-3][:8], ALL, up)
    last_down = lax.ppermute(have[3][8:], ALL, down)
    blocks = [have[offset] for offset, _, _ in SLOTS[:7]] + [last_up, last_down]

    share = jax.ShapeDtypeStruct((XP, QUADS, 32, TEAM * PAIRS), jnp.float32)
    keep, send = pl.pallas_call(
        ladder_kernel,
        in_specs=[pl.BlockSpec(memory_space=pltpu.SMEM)]
        + [pl.BlockSpec(memory_space=pl.ANY)] * (len(SLOTS) + TEAM),
        out_specs=[pl.BlockSpec(memory_space=pltpu.VMEM)] * 2,
        out_shape=(share, share),
        scratch_shapes=[
            pltpu.VMEM((QUADS, YLO, Z, ROWS, PANEL), jnp.bfloat16),
            pltpu.VMEM((QUADS, TEAM * PAIRS, PANEL), jnp.bfloat16),
            pltpu.VMEM((QUADS, TEAM, 32, TEAM * PAIRS), jnp.float32),
            pltpu.SemaphoreType.DMA((1,)),
        ],
        compiler_params=pltpu.CompilerParams(vmem_limit_bytes=24 << 20),
        cost_estimate=pl.CostEstimate(flops=2 << 30, bytes_accessed=10 << 20, transcendentals=0),
        name="ladder",
    )(meta, *blocks, own, swap, across, relay)
    pair = keep + lax.ppermute(send, "core", [(0, 1), (1, 0)])
    summed = (pair[0] + lax.ppermute(pair[1], "xp", [(0, 1), (1, 0)])).astype(jnp.bfloat16)
    pieces = lax.all_to_all(summed, ("yhi", "xh"), 0, 0, tiled=True)
    return pieces.transpose(1, 0, 2).reshape(32, QUADS * TEAM * PAIRS)


def solution(mesh):
    grid = Mesh(mesh.devices.reshape(YLO, Z, YHI, XH, XP, CORE), ALL)
    rows, cols = ("ylo", "z"), ("yhi", "xh", "xp", "core")
    return jax.shard_map(
        compute,
        mesh=grid,
        in_specs=(P(ALL, None), P(ALL, None), P(rows, cols), P(None, cols)),
        out_specs=P(cols, rows),
        check_vma=False,
    )
```

```python
import jax
import jax.numpy as jnp
from jax import lax
from jax.experimental import pallas as pl
from jax.experimental.pallas import tpu as pltpu
from jax.sharding import Mesh, PartitionSpec as P

TILE = 64
YLO, Z, YHI, XH, XP, CORE = 4, 8, 2, 2, 2, 2
Y = YHI * YLO
QUADS = YHI * XH
PANEL = 1024
ROWS = 16
PAIRS = 128
TEAM = XP * CORE
ALL = ("ylo", "z", "yhi", "xh", "xp", "core")


def place(y, z, xh, xp, core):
    return ((((y % YLO * Z + z) * YHI + y // YLO) * XH + xh) * XP + xp) * CORE + core


def plane_groups():
    groups = []
    for xp in range(XP):
        groups += [[place(y, z, xh, xp, 0) for xh in range(XH) for y in range(Y)] for z in range(Z)]
        groups += [[place(y, z, xh, xp, 1) for xh in range(XH) for z in range(Z)] for y in range(Y)]
    return groups


def ring_pairs(parity):
    def partner(at):
        return (at + 1 if at % 2 == parity else at - 1) % 8

    pairs = []
    for xh in range(XH):
        for xp in range(XP):
            for y in range(Y):
                for z in range(Z):
                    pairs.append((place(y, z, xh, xp, 0), place(y, partner(z), xh, xp, 0)))
                    pairs.append((place(y, z, xh, xp, 1), place(partner(y), z, xh, xp, 1)))
    return sorted(pairs)


def spread(tiles):
    tile = lax.broadcasted_iota(jnp.int32, (PANEL // TILE, PANEL), 0)
    lane = lax.broadcasted_iota(jnp.int32, (PANEL // TILE, PANEL), 1)
    picks = (lane // TILE == tile).astype(jnp.bfloat16)
    flags = tiles.astype(jnp.float32).astype(jnp.bfloat16)
    return jnp.dot(flags, picks, preferred_element_type=jnp.float32)


def integral_kernel(meta, ints_hbm, tiles_hbm, out_ref, ints, tiles, sem):
    copies = [
        pltpu.make_async_copy(ints_hbm, ints, sem.at[0]),
        pltpu.make_async_copy(tiles_hbm, tiles, sem.at[1]),
    ]
    for copy in copies:
        copy.start()
    for copy in copies:
        copy.wait()
    wanted = lax.broadcasted_iota(jnp.int32, (8, PANEL // TILE), 0) == meta[2]
    row = jnp.sum(jnp.where(wanted, tiles[...], 0), axis=0, keepdims=True)
    flags = spread(jnp.broadcast_to(row, (8, PANEL // TILE)))[:1]
    masked = (ints[...].astype(jnp.float32) * flags).astype(jnp.bfloat16)
    out_ref[...] = jnp.broadcast_to(masked[None], out_ref.shape)


JOBS = [(n, quad) for n in (2, 3, 0, 1) for quad in range(QUADS)]


def split_kernel(meta, amps, tiles, own, swap, across, taken, dealt, load_sem, store_sem):
    me = meta[3]
    loads, stores = [], []
    for job, (n, quad) in enumerate(JOBS):
        lanes = pl.ds(pl.multiple_of((TEAM * quad + (me ^ n)) * PANEL, PANEL), PANEL)
        loads.append(pltpu.make_async_copy(amps.at[:, lanes], taken.at[job], load_sem.at[job]))
        target = (own.at[quad], swap.at[quad], across.at[0, quad], across.at[1, quad])[n]
        stores.append(pltpu.make_async_copy(dealt.at[job], target, store_sem.at[job]))
    for load in loads:
        load.start()
    for job, (n, quad) in enumerate(JOBS):
        loads[job].wait()
        flags = spread(tiles[TEAM * quad + (me ^ n)])
        for part in range(PAIRS // TILE):
            rows = pl.ds(part * TILE, TILE)
            block = taken[job, rows, :].astype(jnp.float32)
            dealt[job, rows, :] = (block * flags[part : part + 1]).astype(jnp.bfloat16)
        if job:
            stores[job - 1].start()
    stores[-1].start()
    for store in stores:
        store.wait()


def split_amplitudes(meta, amplitudes, tiles):
    shape = (QUADS, PAIRS, PANEL)
    return pl.pallas_call(
        split_kernel,
        in_specs=[
            pl.BlockSpec(memory_space=pltpu.SMEM),
            pl.BlockSpec(memory_space=pltpu.HBM),
            pl.BlockSpec(memory_space=pltpu.VMEM),
        ],
        out_specs=[pl.BlockSpec(memory_space=pltpu.HBM)] * 3,
        out_shape=[jax.ShapeDtypeStruct(s, jnp.bfloat16) for s in (shape, shape, (CORE,) + shape)],
        scratch_shapes=[pltpu.VMEM((len(JOBS), PAIRS, PANEL), jnp.bfloat16)] * 2
        + [pltpu.SemaphoreType.DMA((len(JOBS),))] * 2,
        compiler_params=pltpu.CompilerParams(vmem_limit_bytes=60 << 20),
        cost_estimate=pl.CostEstimate(flops=8 << 20, bytes_accessed=8 << 20, transcendentals=0),
        name="split_amplitudes",
    )(meta, amplitudes, tiles)


MEMBERS = XH * 8
SLOTS = [(offset, 0, MEMBERS) for offset in (0, -1, 1, -2, 2, -3, 3)] + [(4, 0, 8), (4, 8, 8)]


def ladder_kernel(meta, *refs):
    blocks, team = refs[: len(SLOTS)], refs[len(SLOTS) : len(SLOTS) + TEAM]
    keep_ref, send_ref, ints, amps, total, sem = refs[len(SLOTS) + TEAM :]
    core, here, me = meta[0], meta[1], meta[3]
    xp = me // CORE
    sign = 1 - 2 * lax.rem(here, 2)

    def copies(on):
        found = []
        for source, (offset, first, members) in zip(blocks, SLOTS, strict=True):
            there = lax.rem(here + sign * offset + 8, 8)
            for xh in range(first // 8, (first + members) // 8):
                at = xh * 8 - first
                if on == 0:
                    for yhi in range(YHI):
                        found.append((source.at[pl.ds(at + yhi * YLO, YLO)], ints.at[yhi * XH + xh, :, there]))
                else:
                    found.append((source.at[pl.ds(at, Z)], ints.at[(there // YLO) * XH + xh, lax.rem(there, YLO)]))
        return [pltpu.make_async_copy(a, b, sem.at[0]) for a, b in found]

    mine = []
    for n in range(TEAM):
        rows = pl.ds(pl.multiple_of((me ^ n) * PAIRS, PAIRS), PAIRS)
        source = team[n].at[0] if n == 2 else team[n]
        mine.append(pltpu.make_async_copy(source, amps.at[:, rows], sem.at[0]))
    for copy in mine:
        copy.start()
    for on in range(CORE):

        @pl.when(core == on)
        def _():
            todo = copies(on)
            for copy in todo:
                copy.start()
            for copy in todo:
                copy.wait()

    for copy in mine:
        copy.wait()
    for panel in range(QUADS):
        product = lax.dot_general(
            ints[panel].reshape(YLO * Z * ROWS, PANEL),
            amps[panel],
            (((1,), (1,)), ((), ())),
            preferred_element_type=jnp.float32,
        ).reshape(total.shape)
        if panel == 0:
            total[...] = product
        else:
            total[...] += product
    for n in range(XP):
        keep_ref[n] = total[:, (xp ^ n) * CORE + core]
        send_ref[n] = total[:, (xp ^ n) * CORE + 1 - core]


def compute(amplitudes, amp_tiles, integrals, int_tiles):
    core = lax.axis_index("core")
    z = lax.axis_index("z")
    ylo = lax.axis_index("ylo")
    y = lax.axis_index("yhi") * YLO + ylo
    me = lax.axis_index("xp") * CORE + core
    meta = jnp.stack([core, jnp.where(core == 0, z, y), (ylo * Z + z) // 4, me]).astype(jnp.int32)

    panels = pl.pallas_call(
        integral_kernel,
        in_specs=[pl.BlockSpec(memory_space=pltpu.SMEM)] + [pl.BlockSpec(memory_space=pltpu.HBM)] * 2,
        out_specs=pl.BlockSpec(memory_space=pltpu.VMEM),
        out_shape=jax.ShapeDtypeStruct((MEMBERS, ROWS, PANEL), jnp.bfloat16),
        scratch_shapes=[
            pltpu.VMEM((ROWS, PANEL), jnp.bfloat16),
            pltpu.VMEM((8, PANEL // TILE), jnp.int32),
            pltpu.SemaphoreType.DMA((2,)),
        ],
        compiler_params=pltpu.CompilerParams(vmem_limit_bytes=60 << 20),
        name="mask_integrals",
    )(meta, integrals, int_tiles)
    plane = lax.all_to_all(panels, ALL, 0, 0, axis_index_groups=plane_groups(), tiled=True)

    tiles = amp_tiles.reshape(PAIRS // TILE, QUADS * TEAM, PANEL // TILE).transpose(1, 0, 2)
    own, swap, across = split_amplitudes(meta, amplitudes, tiles)
    across = lax.ppermute(across, "xp", [(0, 1), (1, 0)])
    swap = lax.ppermute(swap, "core", [(0, 1), (1, 0)])
    relay = lax.ppermute(across[1], "core", [(0, 1), (1, 0)])

    even, odd = ring_pairs(0), ring_pairs(1)
    have = {0: plane}
    for step in (1, 2, 3):
        have[step] = lax.ppermute(have[1 - step], ALL, even)
        have[-step] = lax.ppermute(have[step - 1], ALL, odd)
    last_odd = lax.ppermute(have[3][:8], ALL, odd)
    last_even = lax.ppermute(have[-3][8:], ALL, even)
    blocks = [have[offset] for offset, _, _ in SLOTS[:7]] + [last_odd, last_even]

    share = jax.ShapeDtypeStruct((XP, QUADS, 32, TEAM * PAIRS), jnp.float32)
    keep, send = pl.pallas_call(
        ladder_kernel,
        in_specs=[pl.BlockSpec(memory_space=pltpu.SMEM)]
        + [pl.BlockSpec(memory_space=pl.ANY)] * (len(SLOTS) + TEAM),
        out_specs=[pl.BlockSpec(memory_space=pltpu.VMEM)] * 2,
        out_shape=(share, share),
        scratch_shapes=[
            pltpu.VMEM((QUADS, YLO, Z, ROWS, PANEL), jnp.bfloat16),
            pltpu.VMEM((QUADS, TEAM * PAIRS, PANEL), jnp.bfloat16),
            pltpu.VMEM((QUADS, TEAM, 32, TEAM * PAIRS), jnp.float32),
            pltpu.SemaphoreType.DMA((1,)),
        ],
        compiler_params=pltpu.CompilerParams(vmem_limit_bytes=24 << 20),
        cost_estimate=pl.CostEstimate(flops=2 << 30, bytes_accessed=10 << 20, transcendentals=0),
        name="ladder",
    )(meta, *blocks, own, swap, across, relay)
    pair = keep + lax.ppermute(send, "core", [(0, 1), (1, 0)])
    summed = (pair[0] + lax.ppermute(pair[1], "xp", [(0, 1), (1, 0)])).astype(jnp.bfloat16)
    pieces = lax.all_to_all(summed, ("yhi", "xh"), 0, 0, tiled=True)
    return pieces.transpose(1, 0, 2).reshape(32, QUADS * TEAM * PAIRS)


def solution(mesh):
    grid = Mesh(mesh.devices.reshape(YLO, Z, YHI, XH, XP, CORE), ALL)
    rows, cols = ("ylo", "z"), ("yhi", "xh", "xp", "core")
    return jax.shard_map(
        compute,
        mesh=grid,
        in_specs=(P(ALL, None), P(ALL, None), P(rows, cols), P(None, cols)),
        out_specs=P(cols, rows),
        check_vma=False,
    )
```

```python
import jax
import jax.numpy as jnp
from jax import lax
from jax.experimental import pallas as pl
from jax.experimental.pallas import tpu as pltpu
from jax.sharding import Mesh, PartitionSpec as P

TILE = 64
YLO, Z, YHI, XH, XP, CORE = 4, 8, 2, 2, 2, 2
Y = YHI * YLO
QUADS = YHI * XH
PANEL = 1024
ROWS = 16
PAIRS = 128
TEAM = XP * CORE
ALL = ("ylo", "z", "yhi", "xh", "xp", "core")


def place(y, z, xh, xp, core):
    return ((((y % YLO * Z + z) * YHI + y // YLO) * XH + xh) * XP + xp) * CORE + core


def plane_groups():
    groups = []
    for xp in range(XP):
        groups += [[place(y, z, xh, xp, 0) for xh in range(XH) for y in range(Y)] for z in range(Z)]
        groups += [[place(y, z, xh, xp, 1) for xh in range(XH) for z in range(Z)] for y in range(Y)]
    return groups


def ring_pairs(parity):
    def partner(at):
        return (at + 1 if at % 2 == parity else at - 1) % 8

    pairs = []
    for xh in range(XH):
        for xp in range(XP):
            for y in range(Y):
                for z in range(Z):
                    pairs.append((place(y, z, xh, xp, 0), place(y, partner(z), xh, xp, 0)))
                    pairs.append((place(y, z, xh, xp, 1), place(partner(y), z, xh, xp, 1)))
    return sorted(pairs)


def spread(tiles):
    tile = lax.broadcasted_iota(jnp.int32, (PANEL // TILE, PANEL), 0)
    lane = lax.broadcasted_iota(jnp.int32, (PANEL // TILE, PANEL), 1)
    picks = (lane // TILE == tile).astype(jnp.bfloat16)
    flags = tiles.astype(jnp.float32).astype(jnp.bfloat16)
    return jnp.dot(flags, picks, preferred_element_type=jnp.float32)


def integral_kernel(meta, ints_hbm, tiles_hbm, out_ref, ints, tiles, sem):
    copies = [
        pltpu.make_async_copy(ints_hbm, ints, sem.at[0]),
        pltpu.make_async_copy(tiles_hbm, tiles, sem.at[1]),
    ]
    for copy in copies:
        copy.start()
    for copy in copies:
        copy.wait()
    wanted = lax.broadcasted_iota(jnp.int32, (8, PANEL // TILE), 0) == meta[2]
    row = jnp.sum(jnp.where(wanted, tiles[...], 0), axis=0, keepdims=True)
    flags = spread(jnp.broadcast_to(row, (8, PANEL // TILE)))[:1]
    masked = (ints[...].astype(jnp.float32) * flags).astype(jnp.bfloat16)
    out_ref[...] = jnp.broadcast_to(masked[None], out_ref.shape)


JOBS = [(n, quad) for n in (2, 3, 0, 1) for quad in range(QUADS)]


def split_kernel(meta, amps, tiles, own, swap, across, taken, dealt, load_sem, store_sem):
    me = meta[3]
    loads, stores = [], []
    for job, (n, quad) in enumerate(JOBS):
        lanes = pl.ds(pl.multiple_of((TEAM * quad + (me ^ n)) * PANEL, PANEL), PANEL)
        loads.append(pltpu.make_async_copy(amps.at[:, lanes], taken.at[job], load_sem.at[job]))
        target = (own.at[quad], swap.at[quad], across.at[0, quad], across.at[1, quad])[n]
        stores.append(pltpu.make_async_copy(dealt.at[job], target, store_sem.at[job]))
    for load in loads:
        load.start()
    width = tiles.shape[1]
    known = jnp.concatenate([tiles[...]] * 4, axis=0)
    for job, (n, quad) in enumerate(JOBS):
        loads[job].wait()
        first = (TEAM * quad + (me ^ n)) * (PANEL // TILE)
        flags = spread(pltpu.roll(known, lax.rem(width - first, width), 1)[:, : PANEL // TILE])
        for part in range(PAIRS // TILE):
            rows = pl.ds(part * TILE, TILE)
            block = taken[job, rows, :].astype(jnp.float32)
            dealt[job, rows, :] = (block * flags[part : part + 1]).astype(jnp.bfloat16)
        if job:
            stores[job - 1].start()
    stores[-1].start()
    for store in stores:
        store.wait()


def split_amplitudes(meta, amplitudes, tiles):
    shape = (QUADS, PAIRS, PANEL)
    return pl.pallas_call(
        split_kernel,
        in_specs=[
            pl.BlockSpec(memory_space=pltpu.SMEM),
            pl.BlockSpec(memory_space=pltpu.HBM),
            pl.BlockSpec(memory_space=pltpu.VMEM),
        ],
        out_specs=[pl.BlockSpec(memory_space=pltpu.HBM)] * 3,
        out_shape=[jax.ShapeDtypeStruct(s, jnp.bfloat16) for s in (shape, shape, (CORE,) + shape)],
        scratch_shapes=[pltpu.VMEM((len(JOBS), PAIRS, PANEL), jnp.bfloat16)] * 2
        + [pltpu.SemaphoreType.DMA((len(JOBS),))] * 2,
        compiler_params=pltpu.CompilerParams(vmem_limit_bytes=60 << 20),
        cost_estimate=pl.CostEstimate(flops=8 << 20, bytes_accessed=8 << 20, transcendentals=0),
        name="split_amplitudes",
    )(meta, amplitudes, tiles)


MEMBERS = XH * 8
SLOTS = [(offset, 0, MEMBERS) for offset in (0, -1, 1, -2, 2, -3, 3)] + [(4, 0, 8), (4, 8, 8)]


def ladder_kernel(meta, *refs):
    blocks, team = refs[: len(SLOTS)], refs[len(SLOTS) : len(SLOTS) + TEAM]
    keep_ref, send_ref, ints, amps, total, sem = refs[len(SLOTS) + TEAM :]
    core, here, me = meta[0], meta[1], meta[3]
    xp = me // CORE
    sign = 1 - 2 * lax.rem(here, 2)

    def copies(on):
        found = []
        for source, (offset, first, members) in zip(blocks, SLOTS, strict=True):
            there = lax.rem(here + sign * offset + 8, 8)
            for xh in range(first // 8, (first + members) // 8):
                at = xh * 8 - first
                if on == 0:
                    for yhi in range(YHI):
                        found.append((source.at[pl.ds(at + yhi * YLO, YLO)], ints.at[yhi * XH + xh, :, there]))
                else:
                    found.append((source.at[pl.ds(at, Z)], ints.at[(there // YLO) * XH + xh, lax.rem(there, YLO)]))
        return [pltpu.make_async_copy(a, b, sem.at[0]) for a, b in found]

    mine = []
    for n in range(TEAM):
        rows = pl.ds(pl.multiple_of((me ^ n) * PAIRS, PAIRS), PAIRS)
        source = team[n].at[0] if n == 2 else team[n]
        mine.append(pltpu.make_async_copy(source, amps.at[:, rows], sem.at[0]))
    for copy in mine:
        copy.start()
    for on in range(CORE):

        @pl.when(core == on)
        def _():
            todo = copies(on)
            for copy in todo:
                copy.start()
            for copy in todo:
                copy.wait()

    for copy in mine:
        copy.wait()
    for panel in range(QUADS):
        product = lax.dot_general(
            ints[panel].reshape(YLO * Z * ROWS, PANEL),
            amps[panel],
            (((1,), (1,)), ((), ())),
            preferred_element_type=jnp.float32,
        ).reshape(total.shape)
        if panel == 0:
            total[...] = product
        else:
            total[...] += product
    for n in range(XP):
        keep_ref[n] = total[:, (xp ^ n) * CORE + core]
        send_ref[n] = total[:, (xp ^ n) * CORE + 1 - core]


def compute(amplitudes, amp_tiles, integrals, int_tiles):
    core = lax.axis_index("core")
    z = lax.axis_index("z")
    ylo = lax.axis_index("ylo")
    y = lax.axis_index("yhi") * YLO + ylo
    me = lax.axis_index("xp") * CORE + core
    meta = jnp.stack([core, jnp.where(core == 0, z, y), (ylo * Z + z) // 4, me]).astype(jnp.int32)

    panels = pl.pallas_call(
        integral_kernel,
        in_specs=[pl.BlockSpec(memory_space=pltpu.SMEM)] + [pl.BlockSpec(memory_space=pltpu.HBM)] * 2,
        out_specs=pl.BlockSpec(memory_space=pltpu.VMEM),
        out_shape=jax.ShapeDtypeStruct((MEMBERS, ROWS, PANEL), jnp.bfloat16),
        scratch_shapes=[
            pltpu.VMEM((ROWS, PANEL), jnp.bfloat16),
            pltpu.VMEM((8, PANEL // TILE), jnp.int32),
            pltpu.SemaphoreType.DMA((2,)),
        ],
        compiler_params=pltpu.CompilerParams(vmem_limit_bytes=60 << 20),
        name="mask_integrals",
    )(meta, integrals, int_tiles)
    plane = lax.all_to_all(panels, ALL, 0, 0, axis_index_groups=plane_groups(), tiled=True)

    own, swap, across = split_amplitudes(meta, amplitudes, amp_tiles)
    across = lax.ppermute(across, "xp", [(0, 1), (1, 0)])
    swap = lax.ppermute(swap, "core", [(0, 1), (1, 0)])
    relay = lax.ppermute(across[1], "core", [(0, 1), (1, 0)])

    even, odd = ring_pairs(0), ring_pairs(1)
    have = {0: plane}
    for step in (1, 2, 3):
        have[step] = lax.ppermute(have[1 - step], ALL, even)
        have[-step] = lax.ppermute(have[step - 1], ALL, odd)
    last_odd = lax.ppermute(have[3][:8], ALL, odd)
    last_even = lax.ppermute(have[-3][8:], ALL, even)
    blocks = [have[offset] for offset, _, _ in SLOTS[:7]] + [last_odd, last_even]

    share = jax.ShapeDtypeStruct((XP, QUADS, 32, TEAM * PAIRS), jnp.float32)
    keep, send = pl.pallas_call(
        ladder_kernel,
        in_specs=[pl.BlockSpec(memory_space=pltpu.SMEM)]
        + [pl.BlockSpec(memory_space=pl.ANY)] * (len(SLOTS) + TEAM),
        out_specs=[pl.BlockSpec(memory_space=pltpu.VMEM)] * 2,
        out_shape=(share, share),
        scratch_shapes=[
            pltpu.VMEM((QUADS, YLO, Z, ROWS, PANEL), jnp.bfloat16),
            pltpu.VMEM((QUADS, TEAM * PAIRS, PANEL), jnp.bfloat16),
            pltpu.VMEM((QUADS, TEAM, 32, TEAM * PAIRS), jnp.float32),
            pltpu.SemaphoreType.DMA((1,)),
        ],
        compiler_params=pltpu.CompilerParams(vmem_limit_bytes=24 << 20),
        cost_estimate=pl.CostEstimate(flops=2 << 30, bytes_accessed=10 << 20, transcendentals=0),
        name="ladder",
    )(meta, *blocks, own, swap, across, relay)
    pair = keep + lax.ppermute(send, "core", [(0, 1), (1, 0)])
    summed = (pair[0] + lax.ppermute(pair[1], "xp", [(0, 1), (1, 0)])).astype(jnp.bfloat16)
    pieces = lax.all_to_all(summed, ("yhi", "xh"), 0, 0, tiled=True)
    return pieces.transpose(1, 0, 2).reshape(32, QUADS * TEAM * PAIRS)


def solution(mesh):
    grid = Mesh(mesh.devices.reshape(YLO, Z, YHI, XH, XP, CORE), ALL)
    rows, cols = ("ylo", "z"), ("yhi", "xh", "xp", "core")
    return jax.shard_map(
        compute,
        mesh=grid,
        in_specs=(P(ALL, None), P(ALL, None), P(rows, cols), P(None, cols)),
        out_specs=P(cols, rows),
        check_vma=False,
    )
```

```python
import jax
import jax.numpy as jnp
from jax import lax
from jax.experimental import pallas as pl
from jax.experimental.pallas import tpu as pltpu
from jax.sharding import Mesh, PartitionSpec as P

TILE = 64
YLO, Z, YHI, XH, XP, CORE = 4, 8, 2, 2, 2, 2
Y = YHI * YLO
QUADS = YHI * XH
PANEL = 1024
ROWS = 16
PAIRS = 128
TEAM = XP * CORE
ALL = ("ylo", "z", "yhi", "xh", "xp", "core")


def place(y, z, xh, xp, core):
    return ((((y % YLO * Z + z) * YHI + y // YLO) * XH + xh) * XP + xp) * CORE + core


def plane_groups():
    groups = []
    for xp in range(XP):
        groups += [[place(y, z, xh, xp, 0) for xh in range(XH) for y in range(Y)] for z in range(Z)]
        groups += [[place(y, z, xh, xp, 1) for xh in range(XH) for z in range(Z)] for y in range(Y)]
    return groups


def ring_pairs(parity):
    def partner(at):
        return (at + 1 if at % 2 == parity else at - 1) % 8

    pairs = []
    for xh in range(XH):
        for xp in range(XP):
            for y in range(Y):
                for z in range(Z):
                    pairs.append((place(y, z, xh, xp, 0), place(y, partner(z), xh, xp, 0)))
                    pairs.append((place(y, z, xh, xp, 1), place(partner(y), z, xh, xp, 1)))
    return sorted(pairs)


def spread(tiles):
    tile = lax.broadcasted_iota(jnp.int32, (PANEL // TILE, PANEL), 0)
    lane = lax.broadcasted_iota(jnp.int32, (PANEL // TILE, PANEL), 1)
    picks = (lane // TILE == tile).astype(jnp.bfloat16)
    flags = tiles.astype(jnp.float32).astype(jnp.bfloat16)
    return jnp.dot(flags, picks, preferred_element_type=jnp.float32)


def integral_kernel(meta, ints_hbm, tiles_hbm, out_ref, ints, tiles, sem):
    copies = [
        pltpu.make_async_copy(ints_hbm, ints, sem.at[0]),
        pltpu.make_async_copy(tiles_hbm, tiles, sem.at[1]),
    ]
    for copy in copies:
        copy.start()
    for copy in copies:
        copy.wait()
    wanted = lax.broadcasted_iota(jnp.int32, (8, PANEL // TILE), 0) == meta[2]
    row = jnp.sum(jnp.where(wanted, tiles[...], 0), axis=0, keepdims=True)
    flags = spread(jnp.broadcast_to(row, (8, PANEL // TILE)))[:1]
    masked = (ints[...].astype(jnp.float32) * flags).astype(jnp.bfloat16)
    out_ref[...] = jnp.broadcast_to(masked[None], out_ref.shape)


JOBS = [(n, quad) for n in (2, 3, 0, 1) for quad in range(QUADS)]


def split_kernel(meta, amps, tiles, own, swap, across, taken, dealt, load_sem, store_sem):
    me = meta[3]
    loads, stores = [], []
    for job, (n, quad) in enumerate(JOBS):
        lanes = pl.ds(pl.multiple_of((TEAM * quad + (me ^ n)) * PANEL, PANEL), PANEL)
        loads.append(pltpu.make_async_copy(amps.at[:, lanes], taken.at[job], load_sem.at[job]))
        target = (own.at[quad], swap.at[quad], across.at[0, quad], across.at[1, quad])[n]
        stores.append(pltpu.make_async_copy(dealt.at[job], target, store_sem.at[job]))
    for load in loads:
        load.start()
    width = tiles.shape[1]
    known = jnp.concatenate([tiles[...]] * 4, axis=0)
    for job, (n, quad) in enumerate(JOBS):
        loads[job].wait()
        first = (TEAM * quad + (me ^ n)) * (PANEL // TILE)
        flags = spread(pltpu.roll(known, lax.rem(width - first, width), 1)[:, : PANEL // TILE])
        for part in range(PAIRS // TILE):
            rows = pl.ds(part * TILE, TILE)
            block = taken[job, rows, :].astype(jnp.float32)
            dealt[job, rows, :] = (block * flags[part : part + 1]).astype(jnp.bfloat16)
        if job:
            stores[job - 1].start()
    stores[-1].start()
    for store in stores:
        store.wait()


def split_amplitudes(meta, amplitudes, tiles):
    shape = (QUADS, PAIRS, PANEL)
    return pl.pallas_call(
        split_kernel,
        in_specs=[
            pl.BlockSpec(memory_space=pltpu.SMEM),
            pl.BlockSpec(memory_space=pltpu.HBM),
            pl.BlockSpec(memory_space=pltpu.VMEM),
        ],
        out_specs=[pl.BlockSpec(memory_space=pltpu.HBM)] * 3,
        out_shape=[jax.ShapeDtypeStruct(s, jnp.bfloat16) for s in (shape, shape, (CORE,) + shape)],
        scratch_shapes=[pltpu.VMEM((len(JOBS), PAIRS, PANEL), jnp.bfloat16)] * 2
        + [pltpu.SemaphoreType.DMA((len(JOBS),))] * 2,
        compiler_params=pltpu.CompilerParams(vmem_limit_bytes=60 << 20),
        cost_estimate=pl.CostEstimate(flops=8 << 20, bytes_accessed=8 << 20, transcendentals=0),
        name="split_amplitudes",
    )(meta, amplitudes, tiles)


MEMBERS = XH * 8
SLOTS = [(offset, 0, MEMBERS) for offset in (0, -1, 1, -2, 2, -3, 3)] + [(4, 0, 8), (4, 8, 8)]


def ladder_kernel(meta, *refs):
    blocks, team = refs[: len(SLOTS)], refs[len(SLOTS) : len(SLOTS) + TEAM]
    keep_ref, send_ref, ints, amps, total, sem = refs[len(SLOTS) + TEAM :]
    core, here, me = meta[0], meta[1], meta[3]
    xp = me // CORE
    sign = 1 - 2 * lax.rem(here, 2)

    def copies(on):
        found = []
        for source, (offset, first, members) in zip(blocks, SLOTS, strict=True):
            there = lax.rem(here + sign * offset + 8, 8)
            for xh in range(first // 8, (first + members) // 8):
                at = xh * 8 - first
                if on == 0:
                    for yhi in range(YHI):
                        found.append((source.at[pl.ds(at + yhi * YLO, YLO)], ints.at[yhi * XH + xh, :, there]))
                else:
                    found.append((source.at[pl.ds(at, Z)], ints.at[(there // YLO) * XH + xh, lax.rem(there, YLO)]))
        return [pltpu.make_async_copy(a, b, sem.at[0]) for a, b in found]

    team_loads = []
    for quad in range(QUADS):
        for n in range(TEAM):
            rows = pl.ds(pl.multiple_of((me ^ n) * PAIRS, PAIRS), PAIRS)
            source = team[n].at[0, quad] if n == 2 else team[n].at[quad]
            team_loads.append(pltpu.make_async_copy(source, amps.at[quad, rows], sem.at[1 + quad]))
    for on in range(CORE):

        @pl.when(core == on)
        def _():
            for copy in copies(on):
                copy.start()

    for copy in team_loads:
        copy.start()
    for on in range(CORE):

        @pl.when(core == on)
        def _():
            for copy in copies(on):
                copy.wait()

    for panel in range(QUADS):
        for copy in team_loads[panel * TEAM : (panel + 1) * TEAM]:
            copy.wait()
        product = lax.dot_general(
            ints[panel].reshape(YLO * Z * ROWS, PANEL),
            amps[panel],
            (((1,), (1,)), ((), ())),
            preferred_element_type=jnp.float32,
        ).reshape(total.shape)
        if panel == 0:
            total[...] = product
        else:
            total[...] += product
    for n in range(XP):
        keep_ref[n] = total[:, (xp ^ n) * CORE + core]
        send_ref[n] = total[:, (xp ^ n) * CORE + 1 - core]


def compute(amplitudes, amp_tiles, integrals, int_tiles):
    core = lax.axis_index("core")
    z = lax.axis_index("z")
    ylo = lax.axis_index("ylo")
    y = lax.axis_index("yhi") * YLO + ylo
    me = lax.axis_index("xp") * CORE + core
    meta = jnp.stack([core, jnp.where(core == 0, z, y), (ylo * Z + z) // 4, me]).astype(jnp.int32)

    panels = pl.pallas_call(
        integral_kernel,
        in_specs=[pl.BlockSpec(memory_space=pltpu.SMEM)] + [pl.BlockSpec(memory_space=pltpu.HBM)] * 2,
        out_specs=pl.BlockSpec(memory_space=pltpu.VMEM),
        out_shape=jax.ShapeDtypeStruct((MEMBERS, ROWS, PANEL), jnp.bfloat16),
        scratch_shapes=[
            pltpu.VMEM((ROWS, PANEL), jnp.bfloat16),
            pltpu.VMEM((8, PANEL // TILE), jnp.int32),
            pltpu.SemaphoreType.DMA((2,)),
        ],
        compiler_params=pltpu.CompilerParams(vmem_limit_bytes=60 << 20),
        name="mask_integrals",
    )(meta, integrals, int_tiles)
    plane = lax.all_to_all(panels, ALL, 0, 0, axis_index_groups=plane_groups(), tiled=True)

    own, swap, across = split_amplitudes(meta, amplitudes, amp_tiles)
    across = lax.ppermute(across, "xp", [(0, 1), (1, 0)])
    swap = lax.ppermute(swap, "core", [(0, 1), (1, 0)])
    relay = lax.ppermute(across[1], "core", [(0, 1), (1, 0)])

    even, odd = ring_pairs(0), ring_pairs(1)
    have = {0: plane}
    for step in (1, 2, 3):
        have[step] = lax.ppermute(have[1 - step], ALL, even)
        have[-step] = lax.ppermute(have[step - 1], ALL, odd)
    last_odd = lax.ppermute(have[3][:8], ALL, odd)
    last_even = lax.ppermute(have[-3][8:], ALL, even)
    blocks = [have[offset] for offset, _, _ in SLOTS[:7]] + [last_odd, last_even]

    share = jax.ShapeDtypeStruct((XP, QUADS, 32, TEAM * PAIRS), jnp.float32)
    keep, send = pl.pallas_call(
        ladder_kernel,
        in_specs=[pl.BlockSpec(memory_space=pltpu.SMEM)]
        + [pl.BlockSpec(memory_space=pl.ANY)] * (len(SLOTS) + TEAM),
        out_specs=[pl.BlockSpec(memory_space=pltpu.VMEM)] * 2,
        out_shape=(share, share),
        scratch_shapes=[
            pltpu.VMEM((QUADS, YLO, Z, ROWS, PANEL), jnp.bfloat16),
            pltpu.VMEM((QUADS, TEAM * PAIRS, PANEL), jnp.bfloat16),
            pltpu.VMEM((QUADS, TEAM, 32, TEAM * PAIRS), jnp.float32),
            pltpu.SemaphoreType.DMA((1 + QUADS,)),
        ],
        compiler_params=pltpu.CompilerParams(vmem_limit_bytes=24 << 20),
        cost_estimate=pl.CostEstimate(flops=2 << 30, bytes_accessed=10 << 20, transcendentals=0),
        name="ladder",
    )(meta, *blocks, own, swap, across, relay)
    pair = keep + lax.ppermute(send, "core", [(0, 1), (1, 0)])
    summed = (pair[0] + lax.ppermute(pair[1], "xp", [(0, 1), (1, 0)])).astype(jnp.bfloat16)
    pieces = lax.all_to_all(summed, ("yhi", "xh"), 0, 0, tiled=True)
    return pieces.transpose(1, 0, 2).reshape(32, QUADS * TEAM * PAIRS)


def solution(mesh):
    grid = Mesh(mesh.devices.reshape(YLO, Z, YHI, XH, XP, CORE), ALL)
    rows, cols = ("ylo", "z"), ("yhi", "xh", "xp", "core")
    return jax.shard_map(
        compute,
        mesh=grid,
        in_specs=(P(ALL, None), P(ALL, None), P(rows, cols), P(None, cols)),
        out_specs=P(cols, rows),
        check_vma=False,
    )
```
